256 devices in a mesh: tok: 4 (over y_lo, core), blk: 64 (over x, z, y_hi).
Axes of the slice: x: 4, y: 4 (y_hi: 2, y_lo: 2; y = y_hi * 2 + y_lo), z: 8, core: 2. Of those that a mesh axis runs over, the one named last changes fastest.
Arguments:
- q_proj: bfloat16 [8192, 2048], P('blk', 'tok'), may hold values from -6 to 6
- k_proj: bfloat16 [8192, 2048], P('blk', 'tok'), may hold values from -6 to 6
- v_proj: bfloat16 [8192, 2048], P('blk', 'tok'), may hold values from -6 to 6
- residual: bfloat16 [8192, 2048], P('blk', 'tok'), may hold values from -6 to 6
- prompt_lengths: int32 [32], replicated, may hold values from 1 to 512, 8192 in all
- expert_ids: int32 [8192, 6], P('blk'), may hold values from 0 to 63, all different within a row; in each aligned block of 128 rows (0 to 127, 128 to 255, ...) at most 24 rows name the same one
- gate_weights: float32 [8192, 6], P('blk'), may hold values from 0.02 to 0.6
- page_table: int32 [512], P('blk'), may hold values from 0 to 511, as said below
- out_weight: bfloat16 [2048, 2048], P('tok'), may hold values from -0.125 to 0.125
- norm_gain: float32 [2048], replicated, may hold values from 0.1 to 1.9
- w_gate: bfloat16 [64, 2048, 1408], P('blk', None, 'tok'), may hold values from -0.125 to 0.125
- w_up: bfloat16 [64, 2048, 1408], P('blk', None, 'tok'), may hold values from -0.125 to 0.125
- w_down: bfloat16 [64, 1408, 2048], P('blk', 'tok'), may hold values from -0.15625 to 0.15625
Outputs:
- layer_out: bfloat16 [8192, 2048], P('blk', 'tok')
- kv_cache: bfloat16 [512, 16, 2, 2048], P('blk', None, None, 'tok')
The draws below stay inside these ranges and needn't reach their ends.
Inputs may be any that keep to these rules, and one draw needn't show every extreme that they name: `prompt_lengths`: the prompts fill the pack of 8192 tokens; the longest has exactly 512 tokens. `expert_ids`: each token names 6 different experts. Among the 128 tokens of one index of blk (aligned blocks) no expert is named by more than 24 tokens, a bound that some block reaches. `page_table`: each aligned block of 8 entries is a permutation of the same block's page numbers.
All inputs are finite; a program needn't handle non-finite values.
Results may differ from the reference program's by a relative error of at most 0.012.
Values may be sent and summed in bfloat16 or wider, within the bound.
A program may use at most 64 MiB of HBM per device.

```python
import math
import jax
import jax.numpy as jnp
import numpy as np
from jax import lax

D = 2048
HEADS = 16
HEAD_DIM = 128
FF = 1408
TOPK = 6
TOK_DEV = 128
PAGE = 16
TOKENS = 8192
HID = 2048
EXPERTS = 64
LMAX = 512
NSEG = 32
CAP = 24
PAGES = 512
PAGES_DEV = 8
N_TOK = 4
N_BLK = 64


def draw_q_proj(key, part):
    base_draw = jnp.clip(jax.random.normal(jax.random.fold_in(key, 1), (TOKENS, HEADS * HEAD_DIM), jnp.float32), -5.0, 5.0)
    return base_draw.astype(jnp.bfloat16)


def draw_k_proj(key, part):
    base_draw = jnp.clip(jax.random.normal(jax.random.fold_in(key, 2), (TOKENS, HEADS * HEAD_DIM), jnp.float32), -5.0, 5.0)
    return base_draw.astype(jnp.bfloat16)


def one_order(block_key):
    return jax.random.permutation(block_key, PAGES_DEV)


def draw_page_table(key, part):
    blocks = TOKENS // TOK_DEV
    keys_all = jax.random.split(key, blocks)
    orders = jax.vmap(one_order)(keys_all)
    return (orders + (jnp.arange(blocks) * PAGES_DEV)[:, None]).reshape(-1).astype(jnp.int32)


def levels(rng, dims, cuts, least, top_value):
    factor_of, own = 1.0, jax.random.fold_in(rng, 6)
    for dim, parts in cuts:
        steps = jnp.exp(jax.random.uniform(jax.random.fold_in(own, dim), (parts,), jnp.float32, least / len(cuts), top_value / len(cuts)))
        factor_of = factor_of * jnp.repeat(steps, dims[dim] // parts).reshape([-1 if axis == dim else 1 for axis in range(len(dims))])
    return factor_of


def length_profile(amount, total, bound, slope):
    weights = [(1 << 20) // math.isqrt(grade ** slope) + 1 for grade in range(2, amount + 1)]
    surplus, given = total - bound - (amount - 1), [1] * (amount - 1)
    while surplus > 0:
        candidates = [i for i in range(amount - 1) if given[i] < bound]
        whole, remaining = sum([weights[i] for i in candidates]), surplus
        for i in candidates:
            more = min(bound - given[i], max(1, remaining * weights[i] // whole), surplus)
            given[i] = given[i] + more
            surplus = surplus - more
    return np.array([bound] + given)


def ragged(stream_key, number_of, total, limit, slope):
    if number_of == 2:
        one = jax.random.randint(stream_key, (), max(1, total - limit), min(limit, total - 1) + 1)
        return jnp.stack([one, total - one])
    tallies = jnp.asarray(length_profile(number_of, total, limit, slope), jnp.int32)
    pairs = (number_of - 1) // 2
    source_of, sink = tallies[1:1 + 2 * pairs:2], tallies[2:2 + 2 * pairs:2]
    room = jnp.minimum(source_of - 1, limit - sink)
    passed = jax.random.randint(jax.random.fold_in(stream_key, 1), (pairs,), 0, 1 << 20) % (room + 1)
    tallies = tallies.at[1:1 + 2 * pairs:2].set(source_of - passed).at[2:2 + 2 * pairs:2].set(sink + passed)
    return tallies[jax.random.permutation(jax.random.fold_in(stream_key, 2), number_of)]


def assign_block(rng, own, number, rows, count, top, most, skew):
    order = jax.random.permutation(rng, count)
    heavy_load, usual = load_shares(count, rows * top, most, skew, True), load_shares(count, rows * top, most, skew, False)
    places = jnp.arange(count)

    def named(tallies, rotation):
        used = int((tallies > 0).sum())
        fixed = max(1, used // 4)
        passed = fixed + (places - fixed + rotation * (used - fixed)) % max(1, count - fixed)
        return jnp.zeros((count,), jnp.int32).at[order[jnp.where(places < fixed, places, passed)]].set(jnp.asarray(tallies, jnp.int32))

    tallies = jnp.where(number % 4 == 0, named(heavy_load, number // 4), named(usual, number - number // 4 - 1))
    mixed = jax.random.permutation(jax.random.fold_in(own, 3), count)
    giver, receiver = mixed[0:count // 2 * 2:2], mixed[1:count // 2 * 2:2]
    room = jnp.minimum(tallies[giver] - 1, most - tallies[receiver]) // 2
    room = jnp.where((giver == order[0]) | (receiver == order[0]) | (tallies[receiver] == 0), 0, jnp.maximum(room, 0))
    passed = jax.random.randint(jax.random.fold_in(own, 4), (count // 2,), 0, 1 << 20) % (room + 1)
    tallies = tallies.at[giver].add(-passed).at[receiver].add(passed)
    labels = jnp.searchsorted(jnp.cumsum(tallies), jnp.arange(rows * top), side="right").astype(jnp.int32)
    grid = labels.reshape(top, rows).T
    grid = grid[jax.random.permutation(jax.random.fold_in(own, 1), rows)]
    rotation = jax.random.randint(jax.random.fold_in(own, 2), (rows, 1), 0, top)
    return jnp.take_along_axis(grid, (jnp.arange(top)[None, :] + rotation) % top, axis=1)


def load_shares(amount, total, most, skew, full):
    loads = [(1 << 20) // math.isqrt(standing ** skew) + 1 for standing in range(1, amount + 1)]
    largest = most if full else min(most, max(-(-total // amount), total * loads[0] // sum(loads)))
    least = 1 if total - largest >= amount - 1 else 0
    given, spare = [largest] + [least] * (amount - 1), total - largest - least * (amount - 1)
    while spare > 0:
        free = [i for i in range(1, amount) if given[i] < largest] or [i for i in range(1, amount) if given[i] < most]
        pool, budget = sum([loads[i] for i in free]), spare
        for i in free:
            more = min(most - given[i], max(1, budget * loads[i] // pool), spare)
            given[i] = given[i] + more
            spare = spare - more
    return np.array(given)


def gaussian(rng, extent, scale, limit, cuts=(), kind=jnp.bfloat16):
    result = jax.random.normal(rng, extent, jnp.float32) * scale
    if len(cuts) > 0:
        result = levels(rng, extent, cuts, -0.22, 0.18) * result
    return jnp.clip(result, min=-limit, max=limit).astype(kind)


def setup_inputs(seed: int = 0) -> dict:
    key_list = jax.random.split(jax.random.key(seed), 14)
    q_proj = draw_q_proj(jax.random.fold_in(key_list[13], 71), 0)
    k_proj = draw_k_proj(jax.random.fold_in(key_list[13], 71), 0)
    v_proj = gaussian(key_list[2], (TOKENS, HID), 1.0, 6.0, ((0, 64), (1, 4)))
    residual = gaussian(key_list[3], (TOKENS, D), 1.0, 6.0, ((0, 64), (1, 4)))
    prompt_lengths = ragged(key_list[4], NSEG, TOKENS, LMAX, 2).astype(jnp.int32)
    expert_ids_keys = jax.random.split(jax.random.fold_in(key_list[5], 1), TOKENS // TOK_DEV)
    expert_ids_turns = jax.random.permutation(jax.random.fold_in(key_list[5], 3), TOKENS // TOK_DEV)
    expert_ids = jax.vmap(lambda own, number: assign_block(jax.random.fold_in(key_list[5], 2), own, number, TOK_DEV, EXPERTS, TOPK, CAP, 2))(expert_ids_keys, expert_ids_turns).reshape((TOKENS, TOPK))
    gate_weights = jnp.clip(jnp.exp(math.log(0.6) - 3.4011974 * jax.random.uniform(key_list[6], (TOKENS, TOPK), jnp.float32) ** levels(key_list[6], (TOKENS, TOPK), ((0, 64),), -0.2, 0.2)), 0.02, 0.6)
    page_table = draw_page_table(jax.random.fold_in(key_list[13], 71), 0)
    out_weight = gaussian(key_list[8], (HID, D), HID ** -0.5, 0.125, ((0, 4),))
    norm_gain = jnp.clip(1.0 + 0.18 * jax.random.normal(key_list[9], (D,), jnp.float32), 0.1, 1.9)
    w_gate = gaussian(key_list[10], (EXPERTS, D, FF), D ** -0.5, 0.125, ((0, 64), (2, 4)))
    w_up = gaussian(key_list[11], (EXPERTS, D, FF), D ** -0.5, 0.125, ((0, 64), (2, 4)))
    w_down = gaussian(key_list[12], (EXPERTS, FF, D), FF ** -0.5, 0.15625, ((0, 64), (1, 4)))
    return dict(q_proj=q_proj, k_proj=k_proj, v_proj=v_proj, residual=residual, prompt_lengths=prompt_lengths, expert_ids=expert_ids, gate_weights=gate_weights, page_table=page_table, out_weight=out_weight, norm_gain=norm_gain, w_gate=w_gate, w_up=w_up, w_down=w_down)


def positions_of(token_ids, prompt_lengths):
    seg_ends = jnp.cumsum(prompt_lengths)
    before = token_ids[:, None] >= seg_ends[None, :]
    segment = lax.optimization_barrier(jnp.sum(before.astype(jnp.int32), axis=1))
    seg_start = lax.optimization_barrier(jnp.max(jnp.where(before, seg_ends[None, :], 0), axis=1))
    return (segment, token_ids - seg_start)

def rotate(block_rows, position):
    row_count = block_rows.shape[0]
    half_dim = HEAD_DIM // 2
    head_view = block_rows.reshape(row_count, -1, HEAD_DIM).astype(jnp.float32)
    inv_freq = 10000.0 ** (-jnp.arange(half_dim, dtype=jnp.float32) / half_dim)
    angles = position.astype(jnp.float32)[:, None] * inv_freq[None, :]
    cosine = jnp.cos(angles)[:, None, :]
    sine_part = jnp.sin(angles)[:, None, :]
    lower_half = head_view[..., :half_dim]
    upper_half = head_view[..., half_dim:]
    turned = jnp.concatenate([lower_half * cosine - upper_half * sine_part, upper_half * cosine + lower_half * sine_part], axis=-1)
    return turned.reshape(row_count, -1).astype(jnp.bfloat16)

def attend(rot_query, key_rows, value_rows, q_seg, q_index, k_seg, k_index):
    q_count = rot_query.shape[0]
    k_count = key_rows.shape[0]
    q_heads = rot_query.reshape(q_count, -1, HEAD_DIM).astype(jnp.float32)
    k_heads = key_rows.reshape(k_count, -1, HEAD_DIM).astype(jnp.float32)
    v_heads = value_rows.reshape(k_count, -1, HEAD_DIM).astype(jnp.float32)
    scores = jnp.einsum('qhd,khd->hqk', q_heads, k_heads) * HEAD_DIM ** (-0.5)
    allowed = (k_seg[None, :] == q_seg[:, None]) & (k_index[None, :] <= q_index[:, None]) & (k_index[None, :] >= 0)
    scores = jnp.where(allowed[None], scores, -1e+30)
    top_score = lax.optimization_barrier(jnp.max(scores, axis=2, keepdims=True))
    exp_terms = jnp.where(allowed[None], jnp.exp(scores - top_score), 0.0)
    soft_weights = (exp_terms / lax.optimization_barrier(jnp.sum(exp_terms, axis=2, keepdims=True))).astype(jnp.bfloat16)
    mixed_heads = jnp.einsum('hqk,khd->qhd', soft_weights.astype(jnp.float32), v_heads)
    return mixed_heads.reshape(q_count, -1).astype(jnp.bfloat16)

def expert_rows(sel_rows, gate_mat, up_mat, down_mat):
    rows_f = sel_rows.astype(jnp.float32)
    gate_act = jnp.dot(rows_f, gate_mat.astype(jnp.float32))
    up_act = jnp.dot(rows_f, up_mat.astype(jnp.float32))
    hidden = (jax.nn.silu(gate_act) * up_act).astype(jnp.bfloat16)
    group = FF // N_TOK
    summed = jnp.zeros((sel_rows.shape[0], D), jnp.float32)
    for member in range(N_TOK):
        piece = jnp.dot(hidden[:, member * group:(member + 1) * group].astype(jnp.float32), down_mat[member * group:(member + 1) * group].astype(jnp.float32))
        summed = summed + piece.astype(jnp.bfloat16).astype(jnp.float32)
    return summed.astype(jnp.bfloat16)

def reference(q_proj, k_proj, v_proj, residual, prompt_lengths, expert_ids, gate_weights, page_table, out_weight, norm_gain, w_gate, w_up, w_down):
    token_ids = jnp.arange(TOKENS, dtype=jnp.int32)
    segment, position = positions_of(token_ids, prompt_lengths)
    rot_query = rotate(q_proj, position)
    rot_keys = rotate(k_proj, position)
    kv_rows = jnp.stack([rot_keys, v_proj], axis=1).reshape(PAGES, PAGE, 2, HID)
    kv_cache = jnp.zeros((PAGES, PAGE, 2, HID), jnp.bfloat16).at[page_table].set(kv_rows)
    pad_keys = jnp.concatenate([jnp.zeros((LMAX, HID), jnp.bfloat16), rot_keys])
    pad_values = jnp.concatenate([jnp.zeros((LMAX, HID), jnp.bfloat16), v_proj])

    def one_block(start):
        q_rows = lax.dynamic_slice_in_dim(rot_query, start, TOK_DEV)
        q_seg = lax.dynamic_slice_in_dim(segment, start, TOK_DEV)
        q_index = lax.dynamic_slice_in_dim(token_ids, start, TOK_DEV)
        key_rows = lax.dynamic_slice_in_dim(pad_keys, start, LMAX + TOK_DEV)
        value_rows = lax.dynamic_slice_in_dim(pad_values, start, LMAX + TOK_DEV)
        key_ids = start - LMAX + jnp.arange(LMAX + TOK_DEV, dtype=jnp.int32)
        key_seg, unused = positions_of(key_ids, prompt_lengths)
        return attend(q_rows, key_rows, value_rows, q_seg, q_index, key_seg, key_ids)
    starts = jnp.arange(TOKENS // TOK_DEV, dtype=jnp.int32) * TOK_DEV
    attention = lax.map(one_block, starts).reshape(TOKENS, HID)
    projected = jnp.dot(attention.astype(jnp.float32), out_weight.astype(jnp.float32))
    stream = (residual.astype(jnp.float32) + projected).astype(jnp.bfloat16)
    wide_rows = stream.astype(jnp.float32)
    inv_scale = lax.rsqrt(lax.optimization_barrier(jnp.mean(wide_rows * wide_rows, axis=1, keepdims=True)) + 1e-06)
    normed = (wide_rows * inv_scale * norm_gain[None, :]).astype(jnp.bfloat16)
    slot_total = N_BLK * CAP

    def one_expert(moe_sum, inputs):
        expert, gate_mat, up_mat, down_mat = inputs
        matches = expert_ids == expert
        weight = lax.optimization_barrier(jnp.sum(jnp.where(matches, gate_weights, 0.0), axis=1))
        chosen = jnp.any(matches, axis=1)
        sel_index = jnp.nonzero(chosen, size=slot_total, fill_value=0)[0].astype(jnp.int32)
        is_valid = jnp.arange(slot_total, dtype=jnp.int32) < jnp.sum(chosen.astype(jnp.int32))
        expert_out = expert_rows(normed[sel_index], gate_mat, up_mat, down_mat)
        scaled = jnp.where(is_valid, weight[sel_index], 0.0)[:, None] * expert_out.astype(jnp.float32)
        return (moe_sum.at[sel_index].add(scaled), None)
    moe, unused = lax.scan(one_expert, jnp.zeros((TOKENS, D), jnp.float32), (jnp.arange(EXPERTS, dtype=jnp.int32), w_gate, w_up, w_down))
    layer_out = (stream.astype(jnp.float32) + moe).astype(jnp.bfloat16)
    return (layer_out, kv_cache)
```

```python
import functools

import jax
import jax.numpy as jnp
from jax import lax
from jax.experimental import pallas as pl
from jax.experimental.pallas import tpu as pltpu
from jax.sharding import PartitionSpec as P

MESH = pl.DeviceIdType.MESH
HEAD_DIM = 128
TOPK = 6
REACH = 4
PAGE = 16
EPSILON = 1e-06

TOK = 128
COLS = 512
WIDTH = 2048
FFL = 352
FFP = 384
CAP = 24
NZ = 8
ROWS = 8 * CAP
F32 = jnp.float32
BF16 = jnp.bfloat16


def place():
    b = lax.axis_index("blk")
    t = lax.axis_index("tok")
    return b // 16, (b // 2) % 8, b % 2, t // 2, t % 2


def dev(x, z, yh, yl, c):
    return {"blk": x * 16 + z * 2 + yh, "tok": yl * 2 + c}


def offset_of(j):
    return -((j + 1) // 2) if j % 2 else j // 2


def mega_kernel(
    lens_ref,
    q_ref,
    k_ref,
    v_ref,
    res_ref,
    table_ref,
    freq_ref,
    gain_ref,
    wo_hbm,
    wg_hbm,
    wu_hbm,
    wd_hbm,
    out_ref,
    krot_ref,
    kv,
    qr,
    mx,
    ls,
    acc,
    att,
    wo,
    rs_out,
    rs_in,
    yo,
    yi,
    zb,
    tb,
    pb,
    pick,
    ph,
    plo,
    sb,
    xb,
    xn,
    gp,
    wgs,
    wus,
    wgu,
    wd,
    hb,
    ob,
    rb,
    mb,
    own_sum,
    swap_out,
    swap_in,
    load_sem,
    kv_send,
    kv_recv,
    rs_sems,
    y_sems,
    tab_send,
    tab_recv,
    ring_send,
    ring_recv,
    wd_send,
    wd_recv,
    s2_send,
    s2_recv,
    self_sem,
    xc_send,
    xc_recv,
    xy_send,
    xy_recv,
    xd_send,
    xd_recv,
    hc_send,
    hc_recv,
    hy_send,
    hy_recv,
    hd_send,
    hd_recv,
    r2_send,
    r2_recv,
    rself_sem,
    m_send,
    m_recv,
    swap_sems,
):
    x, z, yh, yl, c = place()
    h = (yl + yh) % 2
    t_me = yl * 2 + c
    line = yh * 4 + x
    core_peer = dev(x, z, yh, yl, 1 - c)
    y_peer = dev(x, z, yh, 1 - yl, c)
    diag_peer = dev(x, z, yh, 1 - yl, 1 - c)
    t_core, t_y, t_diag = yl * 2 + 1 - c, (1 - yl) * 2 + c, (1 - yl) * 2 + 1 - c
    q_me = h * 2 + c
    q_core, q_y, q_diag = h * 2 + 1 - c, (1 - h) * 2 + c, (1 - h) * 2 + 1 - c
    pair = x * 8 + z
    after, before = (pair + 1) % 32, (pair + 31) % 32
    next_dev = dev(after // 8, after % 8, yh, yl, c)
    prev_dev = dev(before // 8, before % 8, yh, yl, c)
    col_dev = dev(x, z, 1 - yh, yl, c)

    def z_peer(i):
        return dev(x, (z + i) % NZ, yh, yl, c)

    def line_of(i):
        return (line + i) % 8

    def plane_peer(other):
        oyh, ox = other // 4, other % 4
        return dev(ox, z, oyh, (h + oyh) % 2, c)

    def remote(src, dst, ssem, rsem, to):
        return pltpu.make_async_remote_copy(
            src_ref=src, dst_ref=dst, send_sem=ssem, recv_sem=rsem, device_id=to, device_id_type=MESH
        )

    def got(ref, sem):
        pltpu.make_async_copy(ref, ref, sem).wait()

    def dot(a, b):
        return jnp.dot(a, b, preferred_element_type=F32)

    def cols(q, width=COLS, start=0):
        return pl.ds(pl.multiple_of(q * COLS + start, 256), width)

    row_blocks = []
    for q_a, q_b in ((q_y, q_me), (q_diag, q_core)):
        row_blocks += [(q_a, 256, 256), (q_a, 0, 256), (q_b, 0, 512)]
    base = 0
    for q, start, width in row_blocks:
        for src, dst, sem in ((wg_hbm, wgs, 0), (wu_hbm, wus, 1)):
            pltpu.make_async_copy(src.at[0, cols(q, width, start)], dst.at[pl.ds(base, width)], load_sem.at[sem]).start()
        gp[:, base : base + width] = gain_ref[:, cols(q, width, start)]
        base += width
    cp_d = pltpu.make_async_copy(
        wd_hbm.at[0, :, cols(q_me)], wd.at[pl.ds(pl.multiple_of(t_me * FFP, FFP), FFL)], load_sem.at[2]
    )
    cp_d.start()
    cp_o = pltpu.make_async_copy(wo_hbm, wo, load_sem.at[3])
    cp_o.start()

    barrier = pltpu.get_barrier_semaphore()

    def greet(i, carry):
        pl.semaphore_signal(barrier, inc=1, device_id=z_peer(i), device_id_type=MESH)
        pl.semaphore_signal(barrier, inc=1, device_id=plane_peer(line_of(i)), device_id_type=MESH)
        return carry

    lax.fori_loop(1, 8, greet, 0)
    for peer in (core_peer, y_peer, diag_peer, next_dev, prev_dev, col_dev):
        pl.semaphore_signal(barrier, inc=1, device_id=peer, device_id_type=MESH)

    block = pair * 2 + yh
    q_index = block * TOK + lax.broadcasted_iota(jnp.int32, (TOK, TOK), 0)

    def seek(i, carry):
        end, start = carry
        end = end + lens_ref[i]
        return end, jnp.maximum(start, jnp.where(q_index >= end, end, 0))

    _, q_start = lax.fori_loop(0, lens_ref.shape[0], seek, (jnp.int32(0), jnp.zeros((TOK, TOK), jnp.int32)))
    angle = (q_index - q_start).astype(F32) * freq_ref[...]
    cosine = jnp.cos(angle)
    lane = lax.broadcasted_iota(jnp.int32, (TOK, TOK), 1)
    sine = jnp.where(lane < HEAD_DIM // 2, -1.0, 1.0) * jnp.sin(angle)
    for head in range(4):
        s = slice(head * HEAD_DIM, (head + 1) * HEAD_DIM)
        kf = k_ref[:, s].astype(F32)
        turned = (kf * cosine + pltpu.roll(kf, HEAD_DIM // 2, 1) * sine).astype(BF16)
        kv[0, 0, :, s] = turned
        krot_ref[:, s] = turned
    kv[0, 1] = v_ref[...]
    tb[0] = table_ref[...]

    pl.semaphore_wait(barrier, 20)

    def hop(src_slot, dst_slot, n, to):
        return [
            remote(kv.at[src_slot, w], kv.at[dst_slot, w], kv_send.at[n, w], kv_recv.at[dst_slot, w], to)
            for w in range(2)
        ]

    def arrived(slot, w):
        remote(kv.at[slot, w], kv.at[slot, w], kv_send.at[0, w], kv_recv.at[slot, w], prev_dev).wait_recv()

    hop_a = hop(0, 2, 0, next_dev)
    hop_b = hop(2, 4, 1, next_dev)
    hop_own = hop(0, 1, 2, col_dev)
    hop_two = hop(2, 3 - 2 * yh, 3, col_dev)
    hop_four = hop(4, 3, 2, col_dev)
    for w in range(2):
        hop_a[w].start()

    @pl.when(yh == 0)
    def _():
        hop_own[0].start()
        hop_own[1].start()

    tables = []
    for j in range(1, 8):
        cp = remote(tb.at[0], tb.at[j], tab_send.at[j], tab_recv.at[j], z_peer((8 - offset_of(j)) % 8))
        cp.start()
        tables.append(cp)
    wdc = []
    for n, (peer, q) in enumerate(((core_peer, q_core), (y_peer, q_y), (diag_peer, q_diag))):
        cp = remote(
            wd_hbm.at[0, :, cols(q)],
            wd.at[pl.ds(pl.multiple_of(t_me * FFP, FFP), FFL)],
            wd_send.at[n],
            wd_recv.at[n],
            peer,
        )
        cp.start()
        wdc.append(cp)

    for head in range(4):
        s = slice(head * HEAD_DIM, (head + 1) * HEAD_DIM)
        qf = q_ref[:, s].astype(F32)
        qr[:, s] = (qf * cosine + pltpu.roll(qf, HEAD_DIM // 2, 1) * sine).astype(BF16)

    def attend(slot, wait):
        key = (block - slot) * TOK + lane
        allowed = (key <= q_index) & (key >= q_start)
        probs = []
        for head in range(4):
            s = slice(head * HEAD_DIM, (head + 1) * HEAD_DIM)
            score = lax.dot_general(
                qr[:, s], kv[slot, 0, :, s], (((1,), (1,)), ((), ())), preferred_element_type=F32
            ) * (HEAD_DIM**-0.5)
            score = jnp.where(allowed, score, -1e30)
            top = jnp.broadcast_to(jnp.max(score, axis=1, keepdims=True), (TOK, TOK))
            if slot > 0:
                old = mx[head]
                top = jnp.maximum(old, top)
                fade = jnp.exp(old - top)
            e = jnp.where(allowed, jnp.exp(score - top), 0.0)
            line_sum = jnp.broadcast_to(jnp.sum(e, axis=1, keepdims=True), (TOK, TOK))
            mx[head] = top
            if slot > 0:
                ls[head] = ls[head] * fade + line_sum
                acc[head] = acc[head] * fade
            else:
                ls[head] = line_sum
            probs.append(e.astype(BF16))
        if wait:
            wait()
        for head in range(4):
            s = slice(head * HEAD_DIM, (head + 1) * HEAD_DIM)
            mixed = dot(probs[head], kv[slot, 1, :, s])
            if slot > 0:
                acc[head] = acc[head] + mixed
            else:
                acc[head] = mixed

    attend(0, None)

    def prepare_weights():
        got(wgs, load_sem.at[0])
        got(wus, load_sem.at[1])
        zero = jnp.zeros((256, 128), BF16)

        def step(i, carry):
            rows = pl.ds(pl.multiple_of(i * 256, 256), 256)
            wgu[rows, 256:384] = zero
            wgu[rows, 640:768] = zero
            wgu[rows, 0:FFL] = wgs[rows, :]
            wgu[rows, FFP : FFP + FFL] = wus[rows, :]
            return carry

        lax.fori_loop(0, WIDTH // 256, step, 0)
        for t in range(4):
            wd[t * FFP + FFL : (t + 1) * FFP, :] = jnp.zeros((FFP - FFL, COLS), BF16)

    for w in range(2):
        arrived(2, w)
        hop_b[w].start()
        hop_two[w].start()
    attend(2, None)
    prepare_weights()

    expert_col = (
        (lax.broadcasted_iota(jnp.int32, (8, TOK), 0) % 4) * 16
        + z * 2
        + lax.broadcasted_iota(jnp.int32, (8, TOK), 0) // 4
    ).astype(F32)
    upper = (
        lax.broadcasted_iota(jnp.int32, (TOK, TOK), 0) < lax.broadcasted_iota(jnp.int32, (TOK, TOK), 1)
    ).astype(F32).astype(BF16)
    row8 = lax.broadcasted_iota(jnp.int32, (ROWS, 8), 0)
    col8 = lax.broadcasted_iota(jnp.int32, (ROWS, 8), 1)
    spread = ((row8 >= col8 * CAP) & (row8 < col8 * CAP + CAP)).astype(F32).astype(BF16)
    slot_row = (lax.broadcasted_iota(jnp.int32, (ROWS, TOK), 0) % CAP).astype(F32)

    for cp in tables:
        cp.wait_recv()

    def choose(j, carry):
        hit = jnp.zeros((8, TOK), F32)
        weight = jnp.zeros((8, TOK), F32)
        for k in range(TOPK):
            same = jnp.broadcast_to(tb[j, k : k + 1, :], (8, TOK)) == expert_col
            hit = hit + jnp.where(same, 1.0, 0.0)
            weight = weight + jnp.where(same, jnp.broadcast_to(tb[j, 8 + k : 9 + k, :], (8, TOK)), 0.0)
        rank = dot(hit.astype(BF16), upper)
        rank = jnp.where(hit > 0.5, rank, -1.0)
        picked = dot(spread, rank.astype(BF16)) == slot_row
        pick[j] = jnp.where(picked, 1.0, 0.0).astype(BF16)
        w_hi = weight.astype(BF16)
        w_lo = (weight - w_hi.astype(F32)).astype(BF16)
        ph[j] = jnp.where(picked, dot(spread, w_hi), 0.0).astype(BF16)
        plo[j] = jnp.where(picked, dot(spread, w_lo), 0.0).astype(BF16)
        return carry

    lax.fori_loop(0, 8, choose, 0)

    arrived(1, 0)
    attend(1, lambda: arrived(1, 1))

    for w in range(2):
        arrived(4, w)

        @pl.when(yh == 1)
        def _():
            hop_four[w].start()

    attend(4, None)
    arrived(3, 0)
    attend(3, lambda: arrived(3, 1))
    for head in range(4):
        att[:, head * HEAD_DIM : (head + 1) * HEAD_DIM] = (acc[head] / ls[head]).astype(BF16)

    cp_o.wait()
    rs_out[0] = dot(att[...], wo[:, cols(q_core)]).astype(BF16)
    rs_out[1] = dot(att[...], wo[:, cols(q_diag)]).astype(BF16)
    rs_copy = remote(rs_out, rs_in, rs_sems.at[0], rs_sems.at[1], core_peer)
    rs_copy.start()
    resid = res_ref[...].astype(F32)
    high = yh.astype(F32)
    part_y = dot(att[...], wo[:, cols(q_y)]) + resid * high
    part_m = dot(att[...], wo[:, cols(q_me)]) + resid * (1.0 - high)
    rs_copy.wait_recv()
    part_m = part_m + rs_in[0].astype(F32)
    part_y = part_y + rs_in[1].astype(F32)
    yo[:, 0:COLS] = part_y.astype(BF16)
    yo[:, COLS : COLS + 256] = part_m[:, 0:256].astype(BF16)
    y_copy = remote(yo, yi, y_sems.at[0], y_sems.at[1], y_peer)
    y_copy.start()
    y_copy.wait_recv()
    first = yo[:, COLS : COLS + 256].astype(F32) + yi[:, 0:256].astype(F32)
    second = part_m[:, 256:COLS] + yi[:, 256:COLS].astype(F32)
    other = yo[:, 0:256].astype(F32) + yi[:, COLS : COLS + 256].astype(F32)
    zb[0, :, 0:256] = other.astype(BF16)
    zb[0, :, 256:512] = first.astype(BF16)
    zb[0, :, 512:768] = second.astype(BF16)

    right, left = z_peer(1), z_peer(7)
    rings = []

    def ring(j_from, j_to, to):
        cp = remote(zb.at[j_from], zb.at[j_to], ring_send.at[j_to], ring_recv.at[j_to], to)
        cp.start()
        rings.append(cp)

    ring(0, 1, right)
    ring(0, 2, left)

    selfs = {}
    waits = []
    waits_m = {}

    def stage_a(j):
        o = offset_of(j)
        if j > 0:
            remote(zb.at[0], zb.at[j], ring_send.at[j], ring_recv.at[j], left).wait_recv()
            if o < 0 and o > -4:
                ring(j, j + 2, right)
            if o > 0 and o < 3:
                ring(j, j + 2, left)
        sb[j] = dot(pick[j], zb[j]).astype(BF16)
        mine = pl.ds(pl.multiple_of(line * CAP, CAP), CAP)

        def piece(i, carry):
            other = line_of(i)
            remote(
                sb.at[j, pl.ds(pl.multiple_of(other * CAP, CAP), CAP)],
                xb.at[j, mine, pl.ds(256, 768)],
                s2_send.at[j],
                s2_recv.at[j],
                plane_peer(other),
            ).start()
            return carry

        lax.fori_loop(1, 8, piece, 0)
        cp = pltpu.make_async_copy(sb.at[j, mine], xb.at[j, mine, pl.ds(256, 768)], self_sem.at[j])
        cp.start()
        selfs[j] = cp

    def send(src, dst, ssem, rsem, to):
        cp = remote(src, dst, ssem, rsem, to)
        cp.start()
        waits.append(cp)
        return cp

    def stage_b(j):
        selfs[j].wait()
        got(sb.at[j, pl.ds(0, 7 * CAP)], s2_recv.at[j])
        fwd[j] = send(xb.at[j, :, pl.ds(768, 256)], xb.at[j, :, pl.ds(0, 256)], xy_send.at[j], xy_recv.at[j], y_peer)
        direct[j] = send(
            xb.at[j, :, pl.ds(256, 768)], xb.at[j, :, pl.ds(1280, 768)], xc_send.at[j], xc_recv.at[j], core_peer
        )

    fwd, direct, passed, hid_y, hid_c, hid_d = {}, {}, {}, {}, {}, {}

    def stage_c(j):
        fwd[j].wait_recv()
        passed[j] = send(
            xb.at[j, :, pl.ds(0, 256)], xb.at[j, :, pl.ds(1024, 256)], xd_send.at[j], xd_recv.at[j], core_peer
        )

    def hpart(j, t):
        return hb.at[j, :, pl.ds(pl.multiple_of(t * FFP, FFP), FFP)]

    def stage_d(j):
        direct[j].wait_recv()
        passed[j].wait_recv()

        def norm(i, carry):
            rows = pl.ds(pl.multiple_of(i * 32, 32), 32)
            wide = xb[j, rows, :].astype(F32)
            inv = lax.rsqrt(jnp.sum(wide * wide, axis=1, keepdims=True) * (1.0 / WIDTH) + EPSILON)
            xn[rows, :] = (wide * inv * gp[...]).astype(BF16)
            return carry

        lax.fori_loop(0, ROWS // 32, norm, 0)
        act = dot(xn[...], wgu[...])
        gate, up = act[:, :FFP], act[:, FFP:]
        hidden = (gate / (1.0 + jnp.exp(-gate)) * up).astype(BF16)
        hb[j, :, pl.ds(pl.multiple_of(t_me * FFP, FFP), FFP)] = hidden
        hid_y[j] = send(hpart(j, t_me), hpart(j, t_me), hy_send.at[j], hy_recv.at[j], y_peer)
        hid_c[j] = send(hpart(j, t_me), hpart(j, t_me), hc_send.at[j], hc_recv.at[j], core_peer)

    def stage_e(j):
        remote(hpart(j, t_y), hpart(j, t_y), hy_send.at[j], hy_recv.at[j], y_peer).wait_recv()
        hid_d[j] = send(hpart(j, t_y), hpart(j, t_y), hd_send.at[j], hd_recv.at[j], core_peer)

    def stage_f(j):
        if j == 0:
            cp_d.wait()
            for n in range(3):
                wdc[n].wait_recv()
        remote(hpart(j, t_core), hpart(j, t_core), hc_send.at[j], hc_recv.at[j], core_peer).wait_recv()
        remote(hpart(j, t_diag), hpart(j, t_diag), hd_send.at[j], hd_recv.at[j], core_peer).wait_recv()
        ob[j] = dot(hb[j], wd[...]).astype(BF16)
        mine = pl.ds(pl.multiple_of(line * CAP, CAP), CAP)

        def piece(i, carry):
            other = line_of(i)
            remote(
                ob.at[j, pl.ds(pl.multiple_of(other * CAP, CAP), CAP)],
                rb.at[j, mine],
                r2_send.at[j],
                r2_recv.at[j],
                plane_peer(other),
            ).start()
            return carry

        lax.fori_loop(1, 8, piece, 0)
        cp = pltpu.make_async_copy(ob.at[j, mine], rb.at[j, mine], rself_sem.at[j])
        cp.start()
        selfs[8 + j] = cp

    def tdot(a, b):
        return lax.dot_general(a, b, (((0,), (0,)), ((), ())), preferred_element_type=F32)

    def stage_g(j):
        selfs[8 + j].wait()
        got(ob.at[j, pl.ds(0, 7 * CAP)], r2_recv.at[j])
        back = rb[j]
        total = tdot(ph[j], back) + tdot(plo[j], back)
        if j == 0:
            own_sum[...] = total
        else:
            pb[j] = total.astype(BF16)
            cp = remote(pb.at[j], mb.at[j], m_send.at[j], m_recv.at[j], z_peer(offset_of(j) % 8))
            cp.start()
            waits_m[j] = cp

    stages = dict(a=stage_a, b=stage_b, c=stage_c, d=stage_d, e=stage_e, f=stage_f, g=stage_g)
    for step in ORDER.split():
        stages[step[0]](int(step[1]))

    total = own_sum[...]
    for j in range(1, 8):
        waits_m[j].wait_recv()
        total = total + mb[j].astype(F32)
    result = zb[0, :, 256:768].astype(F32) + total

    @pl.when(yh == 0)
    def _():
        out_ref[...] = result

    @pl.when(yh == 1)
    def _():
        swap_out[...] = result.astype(BF16)
        cp = remote(swap_out, swap_in, swap_sems.at[0], swap_sems.at[1], y_peer)
        cp.start()
        cp.wait()
        out_ref[...] = swap_in[...].astype(F32)

    for cp in hop_a + hop_b + hop_two:
        cp.wait_send()

    @pl.when(yh == 0)
    def _():
        for cp in hop_own:
            cp.wait_send()

    @pl.when(yh == 1)
    def _():
        for cp in hop_four:
            cp.wait_send()

    for cp in tables + rings + wdc + waits + [rs_copy, y_copy]:
        cp.wait_send()
    for j in range(1, 8):
        waits_m[j].wait_send()
    for j in range(8):
        got(sb.at[j, pl.ds(0, 7 * CAP)], s2_send.at[j])
        got(ob.at[j, pl.ds(0, 7 * CAP)], r2_send.at[j])


ORDER = (
    "a0 a1 a2 b0 c0 d0 a3 a4 b1 b2 c1 d1 c2 d2 e0 f0 a5 a6 b3 b4 c3 d3 e1 f1 c4 d4 e2 f2 g0 "
    "a7 b5 b6 c5 d5 e3 f3 g1 c6 d6 e4 f4 g2 b7 c7 d7 e5 f5 g3 e6 f6 g4 e7 f7 g5 g6 g7"
)


def mega(lens, q, k, v, res, table, freq, gain, wo, wg, wu, wd):
    vm = pl.BlockSpec(memory_space=pltpu.VMEM)
    sm = pl.BlockSpec(memory_space=pltpu.SMEM)
    anyspace = pl.BlockSpec(memory_space=pl.ANY)
    dma = pltpu.SemaphoreType.DMA
    return pl.pallas_call(
        mega_kernel,
        out_shape=(jax.ShapeDtypeStruct((TOK, COLS), F32), jax.ShapeDtypeStruct((TOK, COLS), BF16)),
        in_specs=[sm] + [vm] * 7 + [anyspace] * 4,
        out_specs=(vm, vm),
        scratch_shapes=[
            pltpu.VMEM((5, 2, TOK, COLS), BF16),
            pltpu.VMEM((TOK, COLS), BF16),
            pltpu.VMEM((4, TOK, TOK), F32),
            pltpu.VMEM((4, TOK, TOK), F32),
            pltpu.VMEM((4, TOK, TOK), F32),
            pltpu.VMEM((TOK, COLS), BF16),
            pltpu.VMEM((COLS, WIDTH), BF16),
            pltpu.VMEM((2, TOK, COLS), BF16),
            pltpu.VMEM((2, TOK, COLS), BF16),
            pltpu.VMEM((TOK, 768), BF16),
            pltpu.VMEM((TOK, 768), BF16),
            pltpu.VMEM((8, TOK, 768), BF16),
            pltpu.VMEM((8, 16, TOK), F32),
            pltpu.VMEM((8, TOK, COLS), BF16),
            pltpu.VMEM((8, ROWS, TOK), BF16),
            pltpu.VMEM((8, ROWS, TOK), BF16),
            pltpu.VMEM((8, ROWS, TOK), BF16),
            pltpu.VMEM((8, ROWS, 768), BF16),
            pltpu.VMEM((8, ROWS, WIDTH), BF16),
            pltpu.VMEM((ROWS, WIDTH), BF16),
            pltpu.VMEM((1, WIDTH), F32),
            pltpu.VMEM((WIDTH, FFL), BF16),
            pltpu.VMEM((WIDTH, FFL), BF16),
            pltpu.VMEM((WIDTH, 2 * FFP), BF16),
            pltpu.VMEM((4 * FFP, COLS), BF16),
            pltpu.VMEM((8, ROWS, 4 * FFP), BF16),
            pltpu.VMEM((8, ROWS, COLS), BF16),
            pltpu.VMEM((8, ROWS, COLS), BF16),
            pltpu.VMEM((8, TOK, COLS), BF16),
            pltpu.VMEM((TOK, COLS), F32),
            pltpu.VMEM((TOK, COLS), BF16),
            pltpu.VMEM((TOK, COLS), BF16),
            dma((4,)),
            dma((4, 2)),
            dma((5, 2)),
            dma((2,)),
            dma((2,)),
            dma((8,)),
            dma((8,)),
            dma((8,)),
            dma((8,)),
            dma((3,)),
            dma((3,)),
        ]
        + [dma((8,)) for _ in range(3)]
        + [dma((8,)) for _ in range(12)]
        + [dma((8,)) for _ in range(5)]
        + [dma((2,))],
        compiler_params=pltpu.CompilerParams(
            collective_id=1, has_side_effects=True, vmem_limit_bytes=58 * 1024 * 1024
        ),
        name="layer",
    )(lens, q, k, v, res, table, freq, gain, wo, wg, wu, wd)


def on_device(
    q_proj,
    k_proj,
    v_proj,
    residual,
    prompt_lengths,
    expert_ids,
    gate_weights,
    page_table,
    out_weight,
    norm_gain,
    w_gate,
    w_up,
    w_down,
):
    half_dim = HEAD_DIM // 2
    inv_freq = 10000.0 ** (-jnp.arange(half_dim, dtype=jnp.float32) / half_dim)
    freq = jnp.concatenate([inv_freq, inv_freq])[None, :]
    pad = jnp.zeros((2, TOK), jnp.float32)
    table = jnp.concatenate([expert_ids.T.astype(jnp.float32), pad, gate_weights.T, pad])
    total, rot_keys = mega(
        prompt_lengths,
        q_proj,
        k_proj,
        v_proj,
        residual,
        table,
        freq,
        norm_gain[None, :],
        out_weight,
        w_gate,
        w_up,
        w_down,
    )
    page_count = TOK // PAGE
    local_page = page_table - lax.axis_index("blk") * page_count
    kv_rows = jnp.stack([rot_keys, v_proj], axis=1).reshape(page_count, PAGE, 2, -1)
    kv_pages = jnp.zeros_like(kv_rows).at[local_page].set(kv_rows)
    return (total.astype(jnp.bfloat16), kv_pages)


def solution(mesh):
    placed = (
        P("blk", "tok"),
        P("blk", "tok"),
        P("blk", "tok"),
        P("blk", "tok"),
        P(),
        P("blk", None),
        P("blk", None),
        P("blk"),
        P("tok", None),
        P(),
        P("blk", None, "tok"),
        P("blk", None, "tok"),
        P("blk", "tok", None),
    )
    return jax.shard_map(
        on_device,
        mesh=mesh,
        in_specs=placed,
        out_specs=(P("blk", "tok"), P("blk", None, None, "tok")),
        check_vma=False,
    )
```
